512 devices in a mesh: row: 32 (over y_lo, z), col: 16 (over x, y_hi, core).
Axes of the slice: x: 4, y: 4 (y_hi: 2, y_lo: 2; y = y_hi * 2 + y_lo), z: 16, core: 2. Of those that a mesh axis runs over, the one named last changes fastest.
Arguments:
- block_ids: int32 [1024, 8], replicated, may hold values from 0 to 767, as said below
- iface_counts: int32 [1024], replicated, may hold values from 6 to 8
- inv_factor: bfloat16 [483328, 472], P(('row', 'col')), as said below
- coupling: bfloat16 [483328, 1024], P(('row', 'col')), may hold values from -0.375 to 0.375
- boundary_block: bfloat16 [24, 4096, 1, 2048], P(None, 'row', None, 'col'), may hold values from -6 to 6
Outputs:
- schur: float32 [24, 4096, 1, 2048], P(None, 'row', None, 'col')
The draws below stay inside these ranges and needn't reach their ends.
Inputs may be any that keep to these rules, and one draw needn't show every extreme that they name: For j < 2, block_ids[s, j] is below 16, equals (s // 2 + j) modulo 16, and is the same for the 2 substructures that share s // 2. Apart from these shared first 2 ids, the ids of the 2 substructures that share s // 2 are distinct modulo 32. `inv_factor`: each substructure's block is lower triangular with a diagonal from 0.5 to 1.5.
All inputs are finite; a program needn't handle non-finite values.
Results may differ from the reference program's by a relative error of at most 0.00044.
Values sent between devices are 32-bit elements; how exact they have to be, the bound alone decides.
No kernel may reach another device: no remote copies, remote signals or barrier semaphores. Data moves between devices by JAX's collectives and lax.ppermute only.
A program may use at most 64 MiB of HBM per device.

```python
import jax
import jax.numpy as jnp
from jax import lax

NI = 472
NB = 8
CS = 2
NQ = 24
CB = 16
SD = 2
SUBS = 1024
CQ = 1
N_ROW = 32
N_COL = 16


def draw_block_ids(key, part):
    places = N_ROW * N_COL
    member = jnp.arange(places, dtype=jnp.int32) % N_COL
    keys = jax.random.split(jax.random.fold_in(key, 11), 3)
    columns = jnp.stack([(member + j) % N_COL for j in range(CS)], axis=1)
    depth = jax.random.randint(keys[0], (places, CS), 0, CB // N_COL)
    span_ids = columns + N_COL * depth
    used = jnp.any((span_ids % N_ROW)[:, :, None] == jnp.arange(N_ROW, dtype=jnp.int32)[None, None, :], axis=1)
    scores = jax.random.randint(keys[1], (places, N_ROW), 0, 2 ** 20) * N_ROW + jnp.arange(N_ROW, dtype=jnp.int32)[None, :]
    scores = scores + used.astype(jnp.int32) * 2 ** 26
    order = jnp.argsort(scores, axis=1)
    owners = order[:, :SD * (NB - CS)].astype(jnp.int32).reshape(places, SD, NB - CS)
    others = owners + N_ROW * jax.random.randint(keys[2], (places, SD, NB - CS), 0, NQ)
    shared = jnp.broadcast_to(span_ids[:, None, :], (places, SD, CS))
    return jnp.concatenate([shared, others], axis=2).reshape(places * SD, NB).astype(jnp.int32)


def draw_inv_factor(key, part):
    subs = SD * N_ROW * N_COL
    first, second = jax.random.split(jax.random.fold_in(key, 23))
    spread = jax.random.normal(first, (subs, NI, NI), jnp.float32)
    lower = jnp.tril(jnp.ones((NI, NI), jnp.float32), -1)
    pivots = jax.random.uniform(second, (subs, NI), jnp.float32, 0.5, 1.5)
    matrix = spread * lower[None] * NI ** (-0.5) + pivots[:, :, None] * jnp.eye(NI, dtype=jnp.float32)[None]
    return matrix.reshape(subs * NI, NI).astype(jnp.bfloat16)


def plant(drawn, own_key, low, top_value):
    spot = [jax.random.randint(jax.random.fold_in(own_key, axis), (), 0, length) for axis, length in enumerate(drawn.shape)]
    widest = drawn.shape.index(max(drawn.shape))
    neighbour = spot[:widest] + [(spot[widest] + 1) % drawn.shape[widest]] + spot[widest + 1:]
    return drawn.at[tuple(spot)].set(low).at[tuple(neighbour)].set(top_value)


def shard_levels(rng, extent, pieces, least, high):
    factor_of = 1.0
    for position, shards_of in pieces:
        steps = jax.random.uniform(jax.random.fold_in(jax.random.fold_in(rng, 6), position), (shards_of,), jnp.float32, least / len(pieces), high / len(pieces))
        factor_of = factor_of * jnp.repeat(jnp.exp(steps), extent[position] // shards_of).reshape((-1,) + (1,) * (len(extent) - 1 - position))
    return factor_of


def noise(own_key, extent, scale, bound, pieces=(), kind=jnp.bfloat16):
    result = jax.random.normal(own_key, extent, jnp.float32) * scale
    if len(pieces) > 0:
        result = shard_levels(own_key, extent, pieces, -0.22, 0.18) * result
    return jnp.clip(result, min=-bound, max=bound).astype(kind)


def setup_inputs(seed: int = 0) -> dict:
    key_list = jax.random.split(jax.random.key(seed), 6)
    block_ids = draw_block_ids(jax.random.fold_in(key_list[5], 71), 0)
    iface_counts = plant(jax.random.randint(key_list[1], (SUBS,), max(CS, NB - 2), NB + 1), jax.random.fold_in(key_list[1], 1), max(CS, NB - 2), NB).astype(jnp.int32)
    inv_factor = draw_inv_factor(jax.random.fold_in(key_list[5], 71), 0)
    coupling = noise(key_list[3], (SUBS * NI, NB * 128), (NI // 2) ** -0.5, 0.375, ((0, 512),))
    boundary_block = noise(key_list[4], (NQ, N_ROW * 128, CQ, N_COL * 128), 1.0, 6.0, ((1, 32), (3, 16)))
    return {"block_ids": block_ids, "iface_counts": iface_counts, "inv_factor": inv_factor, "coupling": coupling, "boundary_block": boundary_block}


def reference(block_ids, iface_counts, inv_factor, coupling, boundary_block):
    subs = SD * N_ROW * N_COL
    factors = inv_factor.reshape(subs, NI, NI)
    couples = coupling.reshape(subs, NI, NB * 128)
    total = jnp.zeros((NQ * N_ROW, 128, CB, 128), jnp.float32)

    def visit(total, item):
        factor, couple, ids, count = item
        mixed = jnp.dot(factor, couple, preferred_element_type=jnp.float32).astype(jnp.bfloat16)
        partial_value = lax.dot_general(mixed, mixed[:, :CS * 128], (((0,), (0,)), ((), ())), preferred_element_type=jnp.float32)
        live = (jnp.arange(NB, dtype=jnp.int32) < count).astype(jnp.float32)
        tiles = partial_value.reshape(NB, 128, CS, 128) * live[:, None, None, None]
        tiles = tiles.transpose(0, 2, 1, 3)
        total = total.at[ids[:, None], :, ids[None, :CS], :].add(tiles)
        return total, None

    total, unused = lax.scan(visit, total, (factors, couples, block_ids, iface_counts))
    dense = total.reshape(NQ * N_ROW * 128, CB * 128)
    given = boundary_block.astype(jnp.float32).reshape(NQ * N_ROW * 128, CB * 128)
    return (given - dense).reshape(NQ, N_ROW * 128, CB // N_COL, N_COL * 128)
```

```python
import functools

import jax
import jax.numpy as jnp
from jax import lax
from jax.experimental import pallas as pl
from jax.experimental.pallas import tpu as pltpu
from jax.sharding import Mesh, PartitionSpec as P

CS = 2
YLO, NZ, XS, YHI, CORE = 2, 16, 4, 2, 2
NCOL = XS * YHI * CORE
PLANE = ("ylo", "x", "yhi", "core")
NPLANE = YLO * NCOL
LIVE = 6
SLOTS = 2 * LIVE + CS
NQ = 24
CAP = 36
FULL = 64
TRASH = NPLANE * NQ
VMEM = pl.BlockSpec(memory_space=pltpu.VMEM)
SMEM = pl.BlockSpec(memory_space=pltpu.SMEM)


def low_half(shape):
    return lax.broadcasted_iota(jnp.int32, shape, 0) % 8 < 4


def slice_kernel(first, second, out):
    low = low_half((128, 128))

    def put(slot, left, right):
        even = jnp.where(low, left, jnp.roll(right.reshape(16, 8, 128), 4, axis=1).reshape(128, 128))
        odd = jnp.where(low, jnp.roll(left.reshape(16, 8, 128), 4, axis=1).reshape(128, 128), right)
        even = even.reshape(16, 8, 128)
        odd = odd.reshape(16, 8, 128)
        for i in range(16):
            out[2 * i, slot] = even[i]
            out[2 * i + 1, slot] = odd[i]

    for member, tiles in enumerate((first, second)):
        for k in range(LIVE):
            rows = pl.ds((CS + k) * 128, 128)
            put(member * LIVE + k, tiles[rows, 0:128], tiles[rows, 128:256])
    for k in range(CS):
        rows = pl.ds(k * 128, 128)
        put(
            2 * LIVE + k,
            first[rows, 0:128] + second[rows, 0:128],
            first[rows, 128:256] + second[rows, 128:256],
        )


def pack_kernel(meta, send_list, slices, *outs):
    me = meta[0]
    for d in range(NZ):
        out = outs[d]

        def body(p, carry, d=d, out=out):
            out[p] = slices[send_list[d * CAP + p]]
            return carry

        lax.fori_loop(0, CAP, body, 0, unroll=4)
        target = lax.rem(me + d, NZ)
        for k in range(CS):
            source = lax.rem(target + NZ - k, NZ)
            out[CAP + k] = (
                slices[source * SLOTS + 2 * LIVE + k]
                + slices[(NCOL + source) * SLOTS + 2 * LIVE + k]
            )


def gather_kernel(meta, recv_list, *refs):
    bufs, total = refs[:NZ], refs[NZ]
    me = meta[0]
    total[...] = jnp.zeros_like(total)
    for d in range(NZ):
        buf = bufs[d]
        base = lax.rem(me + NZ - d, NZ) * CAP
        for k in range(CS):
            spot = lax.rem(me + NZ - k, NZ) * NQ
            total[spot] = total[spot] + buf[CAP + k]

        def body(p, carry, base=base, buf=buf):
            spot = recv_list[base + p]
            total[spot] = total[spot] + buf[p]
            return carry

        lax.fori_loop(0, CAP, body, 0, unroll=4)


def rest_pack_kernel(send_list, slices, out):
    def body(p, carry):
        out[p] = slices[send_list[p]]
        return carry

    lax.fori_loop(0, NZ * (FULL - CAP), body, 0)


def rest_gather_kernel(recv_list, buf, before, total):
    total[...] = before[...]

    def body(p, carry):
        spot = recv_list[p]
        total[spot] = total[spot] + buf[p]
        return carry

    lax.fori_loop(0, NZ * (FULL - CAP), body, 0)


def merge_kernel(total, out):
    low = low_half((8, 128))

    def body(at, carry):
        side = at // NCOL * NCOL
        left = lax.rem(at + NCOL - 1, NCOL) + side
        for h in range(NQ // 2):
            a0 = total[at * NQ + 2 * h]
            a1 = total[at * NQ + 2 * h + 1]
            b0 = total[left * NQ + 2 * h]
            b1 = total[left * NQ + 2 * h + 1]
            out[at, h] = jnp.where(
                low, a0 + jnp.roll(b0, 4, axis=0), jnp.roll(a1, 4, axis=0) + b1
            )
        return carry

    lax.fori_loop(0, NPLANE, body, 0)


def final_kernel(parts, given, out):
    low = low_half((8, 128))

    def body(h, carry):
        for half in range(2):
            base = given[2 * h + half].astype(jnp.float32)
            for i in range(16):
                a = parts[2 * i, h]
                b = parts[2 * i + 1, h]
                if half == 0:
                    tile = jnp.where(low, a, jnp.roll(b, 4, axis=0))
                else:
                    tile = jnp.where(low, jnp.roll(a, 4, axis=0), b)
                out[2 * h + half, 8 * i : 8 * i + 8, :] = base[8 * i : 8 * i + 8] - tile
        return carry

    lax.fori_loop(0, NQ // 2, body, 0)


def lists_of(rank, value, low, high):
    spots = jnp.arange(low, high, dtype=jnp.int32)
    return jnp.sum(
        jnp.where(rank[:, None, :] == spots[None, :, None], value[:, None, :], 0), axis=-1
    )


def on_device(block_ids, iface_counts, inv_factor, coupling, boundary_block):
    me = lax.axis_index("z")
    width = inv_factor.shape[1]
    tiles = []
    for member in range(2):
        rows = slice(member * width, (member + 1) * width)
        mixed = jnp.dot(
            inv_factor[rows], coupling[rows], preferred_element_type=jnp.float32
        ).astype(jnp.bfloat16)
        tiles.append(
            lax.dot_general(
                mixed,
                mixed[:, : CS * 128],
                (((0,), (0,)), ((), ())),
                preferred_element_type=jnp.float32,
            )
        )
    slices = pl.pallas_call(
        slice_kernel,
        out_shape=jax.ShapeDtypeStruct((NPLANE, SLOTS, 8, 128), jnp.float32),
        in_specs=[VMEM, VMEM],
        out_specs=VMEM,
    )(*tiles)
    spread = lax.all_to_all(slices, PLANE, 0, 0, tiled=True).reshape(NPLANE * SLOTS, 8, 128)

    slot = jnp.arange(8, dtype=jnp.int32)
    alive = (slot[None] >= CS) & (slot[None] < iface_counts[:, None])
    key = jnp.where(alive, block_ids, -1)
    key = key.reshape(YLO, NZ, NCOL * 16).transpose(1, 0, 2).reshape(NZ, NPLANE * 16)
    entry = jnp.arange(NPLANE * 16, dtype=jnp.int32)
    plane = jnp.where(key < 0, NZ, key & 15)
    own = lax.dynamic_index_in_dim(plane, me, 0, False)
    step = jnp.arange(NZ, dtype=jnp.int32)
    mask = jnp.concatenate([plane == me, own[None] == ((me + step) % NZ)[:, None]], axis=0)
    before = (entry[:, None] < entry[None, :]).astype(jnp.bfloat16)
    rank = jnp.dot(mask.astype(jnp.bfloat16), before, preferred_element_type=jnp.float32)
    rank = jnp.where(mask, rank.astype(jnp.int32), -1)
    spot = (((key >> 4) & 1) * NCOL + ((entry >> 4) & 15)[None]) * NQ + (key >> 5) - TRASH
    origin = (entry >> 4) * SLOTS + ((entry >> 3) & 1) * LIVE + (entry & 7) - CS
    value = jnp.concatenate([spot, jnp.broadcast_to(origin[None], (NZ, NPLANE * 16))], axis=0)
    table = lists_of(rank, value, 0, CAP)
    recv_list = (table[:NZ] + TRASH).reshape(-1)
    send_list = table[NZ:].reshape(-1)
    load = jnp.sum((plane[:, None, :] == step[None, :, None]).astype(jnp.int32), axis=-1)
    crowded = jnp.max(load) > CAP
    meta = me.astype(jnp.int32).reshape(1)

    packs = pl.pallas_call(
        pack_kernel,
        out_shape=[jax.ShapeDtypeStruct((CAP + CS, 8, 128), jnp.float32)] * NZ,
        in_specs=[SMEM, SMEM, VMEM],
        out_specs=[VMEM] * NZ,
    )(meta, send_list, spread)
    got = [packs[0]]
    for d in range(1, NZ):
        got.append(lax.ppermute(packs[d], "z", [(i, (i + d) % NZ) for i in range(NZ)]))
    total = pl.pallas_call(
        gather_kernel,
        out_shape=jax.ShapeDtypeStruct((TRASH + 1, 8, 128), jnp.float32),
        in_specs=[SMEM, SMEM] + [VMEM] * NZ,
        out_specs=VMEM,
    )(meta, recv_list, *got)

    def rest(total):
        more = lists_of(rank, value, CAP, FULL)
        mine = (more[:NZ] + TRASH).reshape(-1)
        theirs = more[NZ:]
        theirs = jnp.roll(theirs, me, axis=0).reshape(-1)
        buf = pl.pallas_call(
            rest_pack_kernel,
            out_shape=jax.ShapeDtypeStruct((NZ * (FULL - CAP), 8, 128), jnp.float32),
            in_specs=[SMEM, VMEM],
            out_specs=VMEM,
        )(theirs, spread)
        buf = lax.all_to_all(buf, "z", 0, 0, tiled=True)
        return pl.pallas_call(
            rest_gather_kernel,
            out_shape=jax.ShapeDtypeStruct((TRASH + 1, 8, 128), jnp.float32),
            in_specs=[SMEM, VMEM, VMEM],
            out_specs=VMEM,
        )(mine, buf, total)

    total = lax.cond(crowded, rest, lambda total: total, total)
    merged = pl.pallas_call(
        merge_kernel,
        out_shape=jax.ShapeDtypeStruct((NPLANE, NQ // 2, 8, 128), jnp.float32),
        in_specs=[VMEM],
        out_specs=VMEM,
    )(total)
    parts = lax.all_to_all(merged, PLANE, 0, 0, tiled=True)
    result = pl.pallas_call(
        final_kernel,
        out_shape=jax.ShapeDtypeStruct((NQ, 128, 128), jnp.float32),
        in_specs=[VMEM, VMEM],
        out_specs=VMEM,
    )(parts, boundary_block.reshape(NQ, 128, 128))
    return result.reshape(NQ, 128, 1, 128)


def solution(mesh):
    fine = Mesh(mesh.devices.reshape(YLO, NZ, XS, YHI, CORE), ("ylo", "z", "x", "yhi", "core"))
    row, col = ("ylo", "z"), ("x", "yhi", "core")
    return jax.shard_map(
        on_device,
        mesh=fine,
        in_specs=(
            P(),
            P(),
            P(row + col, None),
            P(row + col, None),
            P(None, row, None, col),
        ),
        out_specs=P(None, row, None, col),
        check_vma=False,
    )
```

```python
import functools

import jax
import jax.numpy as jnp
from jax import lax
from jax.experimental import pallas as pl
from jax.experimental.pallas import tpu as pltpu
from jax.sharding import Mesh, PartitionSpec as P

CS = 2
YLO, NZ, XS, YHI, CORE = 2, 16, 4, 2, 2
NCOL = XS * YHI * CORE
PLANE = ("ylo", "x", "yhi", "core")
NPLANE = YLO * NCOL
LIVE = 6
SLOTS = 2 * LIVE + CS
NQ = 24
CAP = 34
FULL = 64
OFFSETS = (0, 8, 7, 9, 6, 10, 5, 11, 4, 12, 3, 13, 2, 14, 1, 15)
TRASH = NPLANE * NQ
VMEM = pl.BlockSpec(memory_space=pltpu.VMEM)
SMEM = pl.BlockSpec(memory_space=pltpu.SMEM)


def low_half(shape):
    return lax.broadcasted_iota(jnp.int32, shape, 0) % 8 < 4


def slice_kernel(first, second, out):
    low = low_half((128, 128))

    def put(slot, left, right):
        even = jnp.where(low, left, jnp.roll(right.reshape(16, 8, 128), 4, axis=1).reshape(128, 128))
        odd = jnp.where(low, jnp.roll(left.reshape(16, 8, 128), 4, axis=1).reshape(128, 128), right)
        even = even.reshape(16, 8, 128)
        odd = odd.reshape(16, 8, 128)
        for i in range(16):
            out[2 * i, slot] = even[i]
            out[2 * i + 1, slot] = odd[i]

    for member, tiles in enumerate((first, second)):
        for k in range(LIVE):
            rows = pl.ds((CS + k) * 128, 128)
            put(member * LIVE + k, tiles[rows, 0:128], tiles[rows, 128:256])
    for k in range(CS):
        rows = pl.ds(k * 128, 128)
        put(
            2 * LIVE + k,
            first[rows, 0:128] + second[rows, 0:128],
            first[rows, 128:256] + second[rows, 128:256],
        )


def pack_kernel(meta, send_list, slices, *outs):
    me = meta[0]
    for at, d in enumerate(OFFSETS):
        out = outs[at]

        def body(p, carry, d=d, out=out):
            out[p] = slices[send_list[d * CAP + p]]
            return carry

        lax.fori_loop(0, CAP, body, 0, unroll=4)
        target = lax.rem(me + d, NZ)
        for k in range(CS):
            source = lax.rem(target + NZ - k, NZ)
            out[CAP + k] = (
                slices[source * SLOTS + 2 * LIVE + k]
                + slices[(NCOL + source) * SLOTS + 2 * LIVE + k]
            )


def gather_kernel(meta, recv_list, *refs):
    bufs, total = refs[:NZ], refs[NZ]
    me = meta[0]
    total[...] = jnp.zeros_like(total)
    for at, d in enumerate(OFFSETS):
        buf = bufs[at]
        base = lax.rem(me + NZ - d, NZ) * CAP
        for k in range(CS):
            spot = lax.rem(me + NZ - k, NZ) * NQ
            total[spot] = total[spot] + buf[CAP + k]

        def body(p, carry, base=base, buf=buf):
            spot = recv_list[base + p]
            total[spot] = total[spot] + buf[p]
            return carry

        lax.fori_loop(0, CAP, body, 0, unroll=4)


def rest_pack_kernel(send_list, slices, out):
    def body(p, carry):
        out[p] = slices[send_list[p]]
        return carry

    lax.fori_loop(0, NZ * (FULL - CAP), body, 0)


def rest_gather_kernel(recv_list, buf, before, total):
    total[...] = before[...]

    def body(p, carry):
        spot = recv_list[p]
        total[spot] = total[spot] + buf[p]
        return carry

    lax.fori_loop(0, NZ * (FULL - CAP), body, 0)


def merge_kernel(total, out):
    low = low_half((8, 128))

    def body(at, carry):
        side = at // NCOL * NCOL
        left = lax.rem(at + NCOL - 1, NCOL) + side
        for h in range(NQ // 2):
            a0 = total[at * NQ + 2 * h]
            a1 = total[at * NQ + 2 * h + 1]
            b0 = total[left * NQ + 2 * h]
            b1 = total[left * NQ + 2 * h + 1]
            out[at, h] = jnp.where(
                low, a0 + jnp.roll(b0, 4, axis=0), jnp.roll(a1, 4, axis=0) + b1
            )
        return carry

    lax.fori_loop(0, NPLANE, body, 0)


def final_kernel(parts, given, out):
    low = low_half((8, 128))

    def body(h, carry):
        for half in range(2):
            base = given[2 * h + half].astype(jnp.float32)
            for i in range(16):
                a = parts[2 * i, h]
                b = parts[2 * i + 1, h]
                if half == 0:
                    tile = jnp.where(low, a, jnp.roll(b, 4, axis=0))
                else:
                    tile = jnp.where(low, jnp.roll(a, 4, axis=0), b)
                out[2 * h + half, 8 * i : 8 * i + 8, :] = base[8 * i : 8 * i + 8] - tile
        return carry

    lax.fori_loop(0, NQ // 2, body, 0)


def lists_of(rank, value, low, high):
    spots = jnp.arange(low, high, dtype=jnp.int32)
    return jnp.sum(
        jnp.where(rank[:, None, :] == spots[None, :, None], value[:, None, :], 0), axis=-1
    )


def on_device(block_ids, iface_counts, inv_factor, coupling, boundary_block):
    me = lax.axis_index("z")
    width = inv_factor.shape[1]
    tiles = []
    for member in range(2):
        rows = slice(member * width, (member + 1) * width)
        mixed = jnp.dot(
            inv_factor[rows], coupling[rows], preferred_element_type=jnp.float32
        ).astype(jnp.bfloat16)
        tiles.append(
            lax.dot_general(
                mixed,
                mixed[:, : CS * 128],
                (((0,), (0,)), ((), ())),
                preferred_element_type=jnp.float32,
            )
        )
    slices = pl.pallas_call(
        slice_kernel,
        out_shape=jax.ShapeDtypeStruct((NPLANE, SLOTS, 8, 128), jnp.float32),
        in_specs=[VMEM, VMEM],
        out_specs=VMEM,
    )(*tiles)
    spread = lax.all_to_all(slices, PLANE, 0, 0, tiled=True).reshape(NPLANE * SLOTS, 8, 128)

    slot = jnp.arange(8, dtype=jnp.int32)
    alive = (slot[None] >= CS) & (slot[None] < iface_counts[:, None])
    key = jnp.where(alive, block_ids, -1)
    key = key.reshape(YLO, NZ, NCOL * 16).transpose(1, 0, 2).reshape(NZ, NPLANE * 16)
    entry = jnp.arange(NPLANE * 16, dtype=jnp.int32)
    plane = jnp.where(key < 0, NZ, key & 15)
    own = lax.dynamic_index_in_dim(plane, me, 0, False)
    step = jnp.arange(NZ, dtype=jnp.int32)
    mask = jnp.concatenate([plane == me, own[None] == ((me + step) % NZ)[:, None]], axis=0)
    before = (entry[:, None] < entry[None, :]).astype(jnp.bfloat16)
    rank = jnp.dot(mask.astype(jnp.bfloat16), before, preferred_element_type=jnp.float32)
    rank = jnp.where(mask, rank.astype(jnp.int32), -1)
    spot = (((key >> 4) & 1) * NCOL + ((entry >> 4) & 15)[None]) * NQ + (key >> 5) - TRASH
    origin = (entry >> 4) * SLOTS + ((entry >> 3) & 1) * LIVE + (entry & 7) - CS
    value = jnp.concatenate([spot, jnp.broadcast_to(origin[None], (NZ, NPLANE * 16))], axis=0)
    table = lists_of(rank, value, 0, CAP)
    recv_list = (table[:NZ] + TRASH).reshape(-1)
    send_list = table[NZ:].reshape(-1)
    load = jnp.sum((plane[:, None, :] == step[None, :, None]).astype(jnp.int32), axis=-1)
    crowded = jnp.max(load) > CAP
    meta = me.astype(jnp.int32).reshape(1)

    packs = pl.pallas_call(
        pack_kernel,
        out_shape=[jax.ShapeDtypeStruct((CAP + CS, 8, 128), jnp.float32)] * NZ,
        in_specs=[SMEM, SMEM, VMEM],
        out_specs=[VMEM] * NZ,
    )(meta, send_list, spread)
    got = [packs[0]]
    for at, d in list(enumerate(OFFSETS))[1:]:
        got.append(lax.ppermute(packs[at], "z", [(i, (i + d) % NZ) for i in range(NZ)]))
    total = pl.pallas_call(
        gather_kernel,
        out_shape=jax.ShapeDtypeStruct((TRASH + 1, 8, 128), jnp.float32),
        in_specs=[SMEM, SMEM] + [VMEM] * NZ,
        out_specs=VMEM,
    )(meta, recv_list, *got)

    def rest(total):
        more = lists_of(rank, value, CAP, FULL)
        mine = (more[:NZ] + TRASH).reshape(-1)
        theirs = more[NZ:]
        theirs = jnp.roll(theirs, me, axis=0).reshape(-1)
        buf = pl.pallas_call(
            rest_pack_kernel,
            out_shape=jax.ShapeDtypeStruct((NZ * (FULL - CAP), 8, 128), jnp.float32),
            in_specs=[SMEM, VMEM],
            out_specs=VMEM,
        )(theirs, spread)
        buf = lax.all_to_all(buf, "z", 0, 0, tiled=True)
        return pl.pallas_call(
            rest_gather_kernel,
            out_shape=jax.ShapeDtypeStruct((TRASH + 1, 8, 128), jnp.float32),
            in_specs=[SMEM, VMEM, VMEM],
            out_specs=VMEM,
        )(mine, buf, total)

    total = lax.cond(crowded, rest, lambda total: total, total)
    merged = pl.pallas_call(
        merge_kernel,
        out_shape=jax.ShapeDtypeStruct((NPLANE, NQ // 2, 8, 128), jnp.float32),
        in_specs=[VMEM],
        out_specs=VMEM,
    )(total)
    parts = lax.all_to_all(merged, PLANE, 0, 0, tiled=True)
    result = pl.pallas_call(
        final_kernel,
        out_shape=jax.ShapeDtypeStruct((NQ, 128, 128), jnp.float32),
        in_specs=[VMEM, VMEM],
        out_specs=VMEM,
    )(parts, boundary_block.reshape(NQ, 128, 128))
    return result.reshape(NQ, 128, 1, 128)


def solution(mesh):
    fine = Mesh(mesh.devices.reshape(YLO, NZ, XS, YHI, CORE), ("ylo", "z", "x", "yhi", "core"))
    row, col = ("ylo", "z"), ("x", "yhi", "core")
    return jax.shard_map(
        on_device,
        mesh=fine,
        in_specs=(
            P(),
            P(),
            P(row + col, None),
            P(row + col, None),
            P(None, row, None, col),
        ),
        out_specs=P(None, row, None, col),
        check_vma=False,
    )
```

```python
import functools

import jax
import jax.numpy as jnp
from jax import lax
from jax.experimental import pallas as pl
from jax.experimental.pallas import tpu as pltpu
from jax.sharding import Mesh, PartitionSpec as P

CS = 2
YLO, NZ, XS, YHI, CORE = 2, 16, 4, 2, 2
NCOL = XS * YHI * CORE
PLANE = ("ylo", "x", "yhi", "core")
NPLANE = YLO * NCOL
LIVE = 6
SLOTS = 2 * LIVE + CS
NQ = 24
CAP = 22
NEAR = 44
LOCAL = 40
FULL = 64
AHEAD = 8
FARTHEST = AHEAD - 1
TRASH = NPLANE * NQ
VMEM = pl.BlockSpec(memory_space=pltpu.VMEM)
SMEM = pl.BlockSpec(memory_space=pltpu.SMEM)


def kernel_call(kernel, limit=16, **rest):
    params = pltpu.CompilerParams(vmem_limit_bytes=limit * 2**20)
    return pl.pallas_call(kernel, compiler_params=params, **rest)


def low_half(shape):
    return lax.broadcasted_iota(jnp.int32, shape, 0) % 8 < 4


def slice_kernel(first, second, out):
    low = low_half((128, 128))

    def put(slot, left, right):
        even = jnp.where(low, left, jnp.roll(right.reshape(16, 8, 128), 4, axis=1).reshape(128, 128))
        odd = jnp.where(low, jnp.roll(left.reshape(16, 8, 128), 4, axis=1).reshape(128, 128), right)
        even = even.reshape(16, 8, 128)
        odd = odd.reshape(16, 8, 128)
        for i in range(16):
            out[2 * i, slot] = even[i]
            out[2 * i + 1, slot] = odd[i]

    for member, tiles in enumerate((first, second)):
        for k in range(LIVE):
            rows = pl.ds((CS + k) * 128, 128)
            put(member * LIVE + k, tiles[rows, 0:128], tiles[rows, 128:256])
    for k in range(CS):
        rows = pl.ds(k * 128, 128)
        put(
            2 * LIVE + k,
            first[rows, 0:128] + second[rows, 0:128],
            first[rows, 128:256] + second[rows, 128:256],
        )


def offset_of(code):
    return code + 1 if code < AHEAD else AHEAD - 1 - code


def shared_slice(slices, target, k):
    source = lax.rem(target + NZ - k, NZ)
    return (
        slices[source * SLOTS + 2 * LIVE + k]
        + slices[(NCOL + source) * SLOTS + 2 * LIVE + k]
    )


def add_rows(count, list_ref, base, src, total):
    def body(p, carry):
        spot = list_ref[base + p]
        total[spot] = total[spot] + src[p]
        return carry

    lax.fori_loop(0, count, body, 0, unroll=2)


def pack_kernel(meta, send_list, slices, out):
    me = meta[0]
    for code in range(NZ - 1):
        target = lax.rem(me + offset_of(code) + NZ, NZ)
        base = target * (CAP + CS)

        def body(p, carry, code=code, base=base):
            out[base + p] = slices[send_list[code * LOCAL + p]]
            return carry

        lax.fori_loop(0, CAP, body, 0, unroll=2)
        for k in range(CS):
            out[base + CAP + k] = shared_slice(slices, target, k)


def relay_kernel(meta, push, kept, send_list, slices, buf, ahead, behind):
    me = meta[0]
    for first, last, row, out in ((0, 8, 16, ahead), (8, 15, 17, behind)):
        step = -1 if first == 0 else 1
        count = push[first]
        base = row * LOCAL

        def own(p, carry, base=base, out=out):
            out[p] = slices[send_list[base + p]]
            return carry

        lax.fori_loop(0, jnp.minimum(count, LOCAL), own, 0)
        for code in range(first + 1, last):
            line = (step * (code - first)) % NZ
            begin = kept[line * NZ + code - 1] + lax.rem(me + line, NZ) * (CAP + CS)
            more = push[line * NZ + code]

            def body(p, carry, out=out, begin=begin, count=count):
                out[count + p] = buf[begin + p]
                return carry

            lax.fori_loop(0, more, body, 0)
            count = count + more


def early_kernel(meta, recv_list, send_list, slices, buf, total):
    me = meta[0]
    total[...] = jnp.zeros_like(total)

    def body(p, carry):
        spot = recv_list[p]
        total[spot] = total[spot] + slices[send_list[15 * LOCAL + p]]
        return carry

    lax.fori_loop(0, LOCAL, body, 0, unroll=2)
    tiles = [shared_slice(slices, me, k) for k in range(CS)]
    for line in range(1, NZ):
        base = lax.rem(me + line, NZ) * (CAP + CS)

        def add(p, carry, base=base, line=line):
            spot = recv_list[line * LOCAL + p]
            total[spot] = total[spot] + buf[base + p]
            return carry

        lax.fori_loop(0, CAP, add, 0, unroll=2)
        tiles = [tile + buf[base + CAP + k] for k, tile in enumerate(tiles)]
    for k in range(CS):
        spot = lax.rem(me + NZ - k, NZ) * NQ
        total[spot] = total[spot] + tiles[k]


def merge(total, out):
    low = low_half((8, 128))

    def body(at, carry):
        side = at // NCOL * NCOL
        left = lax.rem(at + NCOL - 1, NCOL) + side
        for h in range(NQ // 2):
            a0 = total[at * NQ + 2 * h]
            a1 = total[at * NQ + 2 * h + 1]
            b0 = total[left * NQ + 2 * h]
            b1 = total[left * NQ + 2 * h + 1]
            out[at, h] = jnp.where(
                low, a0 + jnp.roll(b0, 4, axis=0), jnp.roll(a1, 4, axis=0) + b1
            )
        return carry

    lax.fori_loop(0, NPLANE, body, 0)


def late_kernel(near_list, ahead, behind, early, out, total):
    total[...] = early[...]
    add_rows(NEAR, near_list, 0, ahead, total)
    add_rows(NEAR, near_list, NEAR, behind, total)
    merge(total, out)


def full_pack_kernel(send_list, slices, out):
    def body(target, carry):
        def inner(p, carry):
            out[target * (FULL + CS) + p] = slices[send_list[target * FULL + p]]
            return carry

        lax.fori_loop(0, FULL, inner, 0)
        for k in range(CS):
            out[target * (FULL + CS) + FULL + k] = shared_slice(slices, target, k)
        return carry

    lax.fori_loop(0, NZ, body, 0)


def full_gather_kernel(meta, recv_list, buf, out, total):
    me = meta[0]
    total[...] = jnp.zeros_like(total)

    def body(source, carry):
        def inner(p, carry):
            spot = recv_list[source * FULL + p]
            total[spot] = total[spot] + buf[source * (FULL + CS) + p]
            return carry

        lax.fori_loop(0, FULL, inner, 0)
        for k in range(CS):
            spot = lax.rem(me + NZ - k, NZ) * NQ
            total[spot] = total[spot] + buf[source * (FULL + CS) + FULL + k]
        return carry

    lax.fori_loop(0, NZ, body, 0)
    merge(total, out)


def final_kernel(parts, given, out):
    low = low_half((8, 128))

    def body(h, carry):
        for half in range(2):
            base = given[2 * h + half].astype(jnp.float32)
            for i in range(16):
                a = parts[2 * i, h]
                b = parts[2 * i + 1, h]
                if half == 0:
                    tile = jnp.where(low, a, jnp.roll(b, 4, axis=0))
                else:
                    tile = jnp.where(low, jnp.roll(a, 4, axis=0), b)
                out[2 * h + half, 8 * i : 8 * i + 8, :] = base[8 * i : 8 * i + 8] - tile
        return carry

    lax.fori_loop(0, NQ // 2, body, 0)


def lists_of(spots, value, count):
    at = jnp.arange(count, dtype=jnp.int32)
    return jnp.sum(
        jnp.where(spots[:, None, :] == at[None, :, None], value[:, None, :], 0), axis=-1
    )


def shape_of(*shape):
    return jax.ShapeDtypeStruct(shape, jnp.float32)


MERGED = shape_of(NPLANE, NQ // 2, 8, 128)
TOTAL = pltpu.VMEM((TRASH + 1, 8, 128), jnp.float32)


def ranks_of(mask, before):
    rank = jnp.dot(mask.astype(jnp.bfloat16), before, preferred_element_type=jnp.float32)
    return rank.astype(jnp.int32)


def on_device(block_ids, iface_counts, inv_factor, coupling, boundary_block):
    me = lax.axis_index("z").astype(jnp.int32)
    width = inv_factor.shape[1]
    tiles = []
    for member in range(2):
        rows = slice(member * width, (member + 1) * width)
        mixed = jnp.dot(
            inv_factor[rows], coupling[rows], preferred_element_type=jnp.float32
        ).astype(jnp.bfloat16)
        tiles.append(
            lax.dot_general(
                mixed,
                mixed[:, : CS * 128],
                (((0,), (0,)), ((), ())),
                preferred_element_type=jnp.float32,
            )
        )
    slices = kernel_call(
        slice_kernel,
        out_shape=shape_of(NPLANE, SLOTS, 8, 128),
        in_specs=[VMEM, VMEM],
        out_specs=VMEM,
    )(*tiles)
    spread = lax.all_to_all(slices, PLANE, 0, 0, tiled=True).reshape(NPLANE * SLOTS, 8, 128)

    slot = jnp.arange(8, dtype=jnp.int32)
    alive = (slot[None] >= CS) & (slot[None] < iface_counts[:, None])
    key = jnp.where(alive, block_ids, -1)
    key = key.reshape(YLO, NZ, NCOL * 16).transpose(1, 0, 2).reshape(NZ, NPLANE * 16)
    key = lax.dynamic_slice_in_dim(jnp.concatenate([key, key], axis=0), me, NZ, 0)
    entry = jnp.arange(NPLANE * 16, dtype=jnp.int32)
    before = (entry[:, None] < entry[None, :]).astype(jnp.bfloat16)
    step = jnp.arange(NZ, dtype=jnp.int32)
    line, code = step[:, None], step[None, :]
    spot = (((key >> 4) & 1) * NCOL + ((entry >> 4) & 15)[None]) * NQ + (key >> 5) - TRASH
    origin = (entry >> 4) * SLOTS + ((entry >> 3) & 1) * LIVE + (entry & 7) - CS
    dead = key < 0
    hop = (key - me - line) & 15
    turn = jnp.where(hop == 0, 15, jnp.where(hop <= AHEAD, hop - 1, 23 - hop))
    turn = jnp.where(dead, -1, turn)
    load = jnp.sum((turn[:, None, :] == step[None, :, None]).astype(jnp.int32), axis=-1)

    inner = (step[:, None] // AHEAD == step[None, :] // AHEAD) & (step[None, :] >= step[:, None])
    extra = jnp.where(code == 15, 0, load) - CAP
    run = jnp.sum(jnp.where(inner[None], extra[:, None, :], 0), axis=-1)
    push = run - jnp.minimum(jnp.min(jnp.where(inner[None], run[:, None, :], 0), axis=-1), 0)
    kept = load - push
    place = step[:, None, None]
    lag = jnp.where(step < AHEAD, -step, step - AHEAD)[None, None, :]
    meets = ((place + lag - step[None, :, None]) & 15) == 0
    near = jnp.where(meets, push[None], 0)
    near_ahead = jnp.sum(jnp.where(code[None] < AHEAD, near, 0), axis=(1, 2))
    near_behind = jnp.sum(jnp.where(code[None] < AHEAD, 0, near), axis=(1, 2))
    crowded = (
        (jnp.min(kept) < 0)
        | (jnp.max(near_ahead) > NEAR)
        | (jnp.max(near_behind) > NEAR)
        | (jnp.max(push) > LOCAL)
        | (jnp.max(jnp.where(code == 15, load, 0)) > LOCAL)
    )

    mine = (key & 15 == me) & ~dead
    sent = turn[0][None] == step[:, None]
    rank = ranks_of(jnp.concatenate([mine, sent], axis=0), before)
    rank_mine, rank_sent = rank[:NZ], rank[NZ:]
    own_code = jnp.where(line == 0, 15, jnp.where(line < 8, 7 + line, 15 - line))
    push_mine = jnp.sum(jnp.where(code == own_code, push, 0), axis=1)
    spots_mine = jnp.where(mine, rank_mine - push_mine[:, None], -1)
    sooner = (line // 8 == code // 8) & jnp.where(line < 8, code < line, code > line)
    base = jnp.sum(jnp.where(sooner, push_mine[None], 0), axis=1)
    spots_near = jnp.where(
        mine & (rank_mine < push_mine[:, None]), base[:, None] + rank_mine, -1
    )
    push_own = push[0][:, None]
    stay = jnp.where(sent & (rank_sent >= push_own), rank_sent - push_own, -1)
    moved = jnp.where(sent & (rank_sent < push_own), rank_sent, -1)
    above = jnp.concatenate([moved[1:], moved[:1]], axis=0)
    rides = (above >= 0) & (line != FARTHEST) & (line < 14)
    spots_sent = jnp.where(rides, kept[0][:, None] + above, stay)
    table = lists_of(
        jnp.concatenate([spots_mine, spots_sent, moved[:1], moved[8:9]], axis=0),
        jnp.concatenate([spot, jnp.broadcast_to(origin[None], (NZ + 2, NPLANE * 16))], axis=0),
        LOCAL,
    )
    recv_list = (table[:NZ] + TRASH).reshape(-1)
    send_list = table[NZ:].reshape(-1)
    at = jnp.arange(NEAR, dtype=jnp.int32)[:, None, None]
    near_hits = jnp.where(spots_near[None] == at, spot[None], 0)
    near_list = (
        jnp.stack([jnp.sum(near_hits[:, 8:], axis=(1, 2)), jnp.sum(near_hits[:, :8], axis=(1, 2))])
        + TRASH
    ).reshape(-1)
    push_flat, kept_flat = push.reshape(-1), kept.reshape(-1)
    recv_list, send_list, near_list, push_flat, kept_flat, crowded = lax.optimization_barrier(
        (recv_list, send_list, near_list, push_flat, kept_flat, crowded)
    )
    meta = me.reshape(1)

    def fast(spread):
        buf = kernel_call(
            pack_kernel,
            out_shape=shape_of(NZ * (CAP + CS), 8, 128),
            in_specs=[SMEM, SMEM, VMEM],
            out_specs=VMEM,
        )(meta, send_list, spread)
        buf = lax.all_to_all(buf, "z", 0, 0, tiled=True)
        ahead, behind = kernel_call(
            relay_kernel,
            out_shape=[shape_of(NEAR, 8, 128)] * 2,
            in_specs=[SMEM] * 4 + [VMEM] * 2,
            out_specs=[VMEM] * 2,
        )(meta, push_flat, kept_flat, send_list, spread, buf)
        ahead = lax.ppermute(ahead, "z", [(i, (i + 1) % NZ) for i in range(NZ)])
        behind = lax.ppermute(behind, "z", [(i, (i - 1) % NZ) for i in range(NZ)])
        total = kernel_call(
            early_kernel,
            out_shape=shape_of(TRASH + 1, 8, 128),
            in_specs=[SMEM] * 3 + [VMEM] * 2,
            out_specs=VMEM,
        )(meta, recv_list, send_list, spread, buf)
        return kernel_call(
            late_kernel,
            out_shape=MERGED,
            in_specs=[SMEM] + [VMEM] * 3,
            out_specs=VMEM,
            scratch_shapes=[TOTAL],
        )(near_list, ahead, behind, total)

    def full(spread):
        plane = jnp.where(dead, NZ, key & 15)
        mask = jnp.concatenate([mine, plane[0][None] == step[:, None]], axis=0)
        spots = jnp.where(mask, ranks_of(mask, before), -1)
        value = jnp.concatenate([spot, jnp.broadcast_to(origin[None], spot.shape)], axis=0)
        lists = lists_of(spots, value, FULL)
        theirs = lists[NZ:].reshape(-1)
        ours = (jnp.roll(lists[:NZ], me, axis=0) + TRASH).reshape(-1)
        buf = kernel_call(
            full_pack_kernel,
            out_shape=shape_of(NZ * (FULL + CS), 8, 128),
            in_specs=[SMEM, VMEM],
            out_specs=VMEM,
        )(theirs, spread)
        buf = lax.all_to_all(buf, "z", 0, 0, tiled=True)
        return kernel_call(
            full_gather_kernel,
            out_shape=MERGED,
            in_specs=[SMEM, SMEM, VMEM],
            out_specs=VMEM,
            scratch_shapes=[TOTAL],
        )(meta, ours, buf)

    merged = lax.cond(crowded, full, fast, spread)
    parts = lax.all_to_all(merged, PLANE, 0, 0, tiled=True)
    result = kernel_call(
        final_kernel,
        out_shape=shape_of(NQ, 128, 128),
        in_specs=[VMEM, VMEM],
        out_specs=VMEM,
    )(parts, boundary_block.reshape(NQ, 128, 128))
    return result.reshape(NQ, 128, 1, 128)


def solution(mesh):
    fine = Mesh(mesh.devices.reshape(YLO, NZ, XS, YHI, CORE), ("ylo", "z", "x", "yhi", "core"))
    row, col = ("ylo", "z"), ("x", "yhi", "core")
    return jax.shard_map(
        on_device,
        mesh=fine,
        in_specs=(
            P(),
            P(),
            P(row + col, None),
            P(row + col, None),
            P(None, row, None, col),
        ),
        out_specs=P(None, row, None, col),
        check_vma=False,
    )
```

```python
import functools

import jax
import jax.numpy as jnp
from jax import lax
from jax.experimental import pallas as pl
from jax.experimental.pallas import tpu as pltpu
from jax.sharding import Mesh, PartitionSpec as P

CS = 2
YLO, NZ, XS, YHI, CORE = 2, 16, 4, 2, 2
NCOL = XS * YHI * CORE
PLANE = ("ylo", "x", "yhi", "core")
NPLANE = YLO * NCOL
LIVE = 6
SLOTS = 2 * LIVE + CS
NQ = 24
CAP = 22
NEAR = 64
LOCAL = 40
FULL = 64
TRASH = NPLANE * NQ
VMEM = pl.BlockSpec(memory_space=pltpu.VMEM)
SMEM = pl.BlockSpec(memory_space=pltpu.SMEM)


def kernel_call(kernel, limit=16, **rest):
    params = pltpu.CompilerParams(vmem_limit_bytes=limit * 2**20)
    return pl.pallas_call(kernel, compiler_params=params, **rest)


def low_half(shape):
    return lax.broadcasted_iota(jnp.int32, shape, 0) % 8 < 4


def slice_kernel(first, second, out):
    low = low_half((128, 128))

    def put(slot, left, right):
        even = jnp.where(low, left, jnp.roll(right.reshape(16, 8, 128), 4, axis=1).reshape(128, 128))
        odd = jnp.where(low, jnp.roll(left.reshape(16, 8, 128), 4, axis=1).reshape(128, 128), right)
        even = even.reshape(16, 8, 128)
        odd = odd.reshape(16, 8, 128)
        for i in range(16):
            out[2 * i, slot] = even[i]
            out[2 * i + 1, slot] = odd[i]

    for member, tiles in enumerate((first, second)):
        for k in range(LIVE):
            rows = pl.ds((CS + k) * 128, 128)
            put(member * LIVE + k, tiles[rows, 0:128], tiles[rows, 128:256])
    for k in range(CS):
        rows = pl.ds(k * 128, 128)
        put(
            2 * LIVE + k,
            first[rows, 0:128] + second[rows, 0:128],
            first[rows, 128:256] + second[rows, 128:256],
        )


def shared_slice(slices, target, k):
    source = lax.rem(target + NZ - k, NZ)
    return (
        slices[source * SLOTS + 2 * LIVE + k]
        + slices[(NCOL + source) * SLOTS + 2 * LIVE + k]
    )


def pack_kernel(meta, send_list, slices, out):
    me = meta[0]
    for code in range(NZ - 1):
        target = lax.rem(me + code + 1, NZ)
        base = target * (CAP + CS)

        def body(p, carry, code=code, base=base):
            out[base + p] = slices[send_list[code * LOCAL + p]]
            return carry

        lax.fori_loop(0, CAP, body, 0, unroll=True)
        for k in range(CS):
            out[base + CAP + k] = shared_slice(slices, target, k)


def relay_kernel(meta, push, kept, send_list, slices, buf, out):
    me = meta[0]
    count = push[0]

    def own(p, carry):
        out[p] = slices[send_list[NZ * LOCAL + p]]
        return carry

    lax.fori_loop(0, count, own, 0)
    for code in range(1, NZ - 1):
        line = NZ - code
        begin = kept[line * NZ + code - 1] + lax.rem(me + line, NZ) * (CAP + CS)
        more = push[line * NZ + code]

        def body(p, carry, begin=begin, count=count):
            out[count + p] = buf[begin + p]
            return carry

        lax.fori_loop(0, more, body, 0)
        count = count + more


def early_kernel(meta, recv_list, send_list, slices, buf, out, total):
    me = meta[0]
    total[...] = jnp.zeros_like(total)

    def body(p, carry):
        spot = recv_list[p]
        total[spot] = total[spot] + slices[send_list[15 * LOCAL + p]]
        return carry

    lax.fori_loop(0, LOCAL, body, 0, unroll=2)
    tiles = [shared_slice(slices, me, k) for k in range(CS)]
    for line in range(1, NZ):
        base = lax.rem(me + line, NZ) * (CAP + CS)

        def add(p, carry, base=base, line=line):
            spot = recv_list[line * LOCAL + p]
            total[spot] = total[spot] + buf[base + p]
            return carry

        lax.fori_loop(0, CAP, add, 0, unroll=2)
        tiles = [tile + buf[base + CAP + k] for k, tile in enumerate(tiles)]
    for k in range(CS):
        spot = lax.rem(me + NZ - k, NZ) * NQ
        total[spot] = total[spot] + tiles[k]
    merge(total, out)


def merge(total, out):
    low = low_half((8, 128))

    def body(at, carry):
        side = at // NCOL * NCOL
        left = lax.rem(at + NCOL - 1, NCOL) + side
        for h in range(NQ // 2):
            a0 = total[at * NQ + 2 * h]
            a1 = total[at * NQ + 2 * h + 1]
            b0 = total[left * NQ + 2 * h]
            b1 = total[left * NQ + 2 * h + 1]
            out[at, h] = jnp.where(
                low, a0 + jnp.roll(b0, 4, axis=0), jnp.roll(a1, 4, axis=0) + b1
            )
        return carry

    lax.fori_loop(0, NPLANE, body, 0)


def late_kernel(meta, near_list, near, early, out):
    out[...] = early[...]
    side = lax.broadcasted_iota(jnp.int32, (8, 128), 0) // 4

    def body(p, carry):
        spot = near_list[p]
        at, q = spot // NQ, spot % NQ
        h, odd = q // 2, q % 2
        right = at // NCOL * NCOL + (at + 1) % NCOL
        tile = near[p]
        turned = jnp.roll(tile, 4, axis=0)
        keep = side == odd
        first = jnp.where(odd == 0, tile, turned)
        second = jnp.where(odd == 0, turned, tile)
        out[at, h] = out[at, h] + jnp.where(keep, first, 0.0)
        out[right, h] = out[right, h] + jnp.where(keep, second, 0.0)
        return carry

    lax.fori_loop(0, meta[1], body, 0)


def full_pack_kernel(send_list, slices, out):
    def body(target, carry):
        def inner(p, carry):
            out[target * (FULL + CS) + p] = slices[send_list[target * FULL + p]]
            return carry

        lax.fori_loop(0, FULL, inner, 0)
        for k in range(CS):
            out[target * (FULL + CS) + FULL + k] = shared_slice(slices, target, k)
        return carry

    lax.fori_loop(0, NZ, body, 0)


def full_gather_kernel(meta, recv_list, buf, out, total):
    me = meta[0]
    total[...] = jnp.zeros_like(total)

    def body(source, carry):
        def inner(p, carry):
            spot = recv_list[source * FULL + p]
            total[spot] = total[spot] + buf[source * (FULL + CS) + p]
            return carry

        lax.fori_loop(0, FULL, inner, 0)
        for k in range(CS):
            spot = lax.rem(me + NZ - k, NZ) * NQ
            total[spot] = total[spot] + buf[source * (FULL + CS) + FULL + k]
        return carry

    lax.fori_loop(0, NZ, body, 0)
    merge(total, out)


def final_kernel(parts, given, out):
    low = low_half((8, 128))

    def body(h, carry):
        for half in range(2):
            base = given[2 * h + half].astype(jnp.float32)
            for i in range(16):
                a = parts[2 * i, h]
                b = parts[2 * i + 1, h]
                if half == 0:
                    tile = jnp.where(low, a, jnp.roll(b, 4, axis=0))
                else:
                    tile = jnp.where(low, jnp.roll(a, 4, axis=0), b)
                out[2 * h + half, 8 * i : 8 * i + 8, :] = base[8 * i : 8 * i + 8] - tile
        return carry

    lax.fori_loop(0, NQ // 2, body, 0)


def lists_of(spots, value, count):
    at = jnp.arange(count, dtype=jnp.int32)
    return jnp.sum(
        jnp.where(spots[:, None, :] == at[None, :, None], value[:, None, :], 0), axis=-1
    )


def shape_of(*shape):
    return jax.ShapeDtypeStruct(shape, jnp.float32)


MERGED = shape_of(NPLANE, NQ // 2, 8, 128)
TOTAL = pltpu.VMEM((TRASH + 1, 8, 128), jnp.float32)


def ranks_of(mask, before):
    rank = jnp.dot(mask.astype(jnp.bfloat16), before, preferred_element_type=jnp.float32)
    return rank.astype(jnp.int32)


def on_device(block_ids, iface_counts, inv_factor, coupling, boundary_block):
    me = lax.axis_index("z").astype(jnp.int32)
    width = inv_factor.shape[1]
    tiles = []
    for member in range(2):
        rows = slice(member * width, (member + 1) * width)
        mixed = jnp.dot(
            inv_factor[rows], coupling[rows], preferred_element_type=jnp.float32
        ).astype(jnp.bfloat16)
        tiles.append(
            lax.dot_general(
                mixed,
                mixed[:, : CS * 128],
                (((0,), (0,)), ((), ())),
                preferred_element_type=jnp.float32,
            )
        )
    slices = kernel_call(
        slice_kernel,
        out_shape=shape_of(NPLANE, SLOTS, 8, 128),
        in_specs=[VMEM, VMEM],
        out_specs=VMEM,
    )(*tiles)
    spread = lax.all_to_all(slices, PLANE, 0, 0, tiled=True).reshape(NPLANE * SLOTS, 8, 128)

    slot = jnp.arange(8, dtype=jnp.int32)
    alive = (slot[None] >= CS) & (slot[None] < iface_counts[:, None])
    key = jnp.where(alive, block_ids, -1)
    key = key.reshape(YLO, NZ, NCOL * 16).transpose(1, 0, 2).reshape(NZ, NPLANE * 16)
    key = lax.dynamic_slice_in_dim(jnp.concatenate([key, key], axis=0), me, NZ, 0)
    entry = jnp.arange(NPLANE * 16, dtype=jnp.int32)
    before = (entry[:, None] < entry[None, :]).astype(jnp.bfloat16)
    step = jnp.arange(NZ, dtype=jnp.int32)
    line, code = step[:, None], step[None, :]
    spot = (((key >> 4) & 1) * NCOL + ((entry >> 4) & 15)[None]) * NQ + (key >> 5) - TRASH
    origin = (entry >> 4) * SLOTS + ((entry >> 3) & 1) * LIVE + (entry & 7) - CS
    dead = key < 0
    hop = (key - me - line) & 15
    turn = jnp.where(dead, -1, (hop - 1) & 15)
    load = jnp.sum((turn[:, None, :] == step[None, :, None]).astype(jnp.int32), axis=-1)

    inner = step[None, :] >= step[:, None]
    extra = jnp.where(code == 15, 0, load) - CAP
    run = jnp.sum(jnp.where(inner[None], extra[:, None, :], 0), axis=-1)
    push = run - jnp.minimum(jnp.min(jnp.where(inner[None], run[:, None, :], 0), axis=-1), 0)
    kept = load - push
    place = step[:, None, None]
    meets = ((place - step[None, None, :] - step[None, :, None]) & 15) == 0
    near = jnp.sum(jnp.where(meets, push[None], 0), axis=(1, 2))
    crowded = (
        (jnp.min(kept) < 0)
        | (jnp.max(near) > NEAR)
        | (jnp.max(push) > LOCAL)
        | (jnp.max(jnp.where(code == 15, load, 0)) > LOCAL)
    )

    mine = (key & 15 == me) & ~dead
    sent = turn[0][None] == step[:, None]
    rank = ranks_of(jnp.concatenate([mine, sent], axis=0), before)
    rank_mine, rank_sent = rank[:NZ], rank[NZ:]
    push_mine = jnp.sum(jnp.where(code == 15 - line, push, 0), axis=1)
    spots_mine = jnp.where(mine, rank_mine - push_mine[:, None], -1)
    base = jnp.sum(jnp.where(code > line, push_mine[None], 0), axis=1)
    spots_near = jnp.where(
        mine & (rank_mine < push_mine[:, None]), base[:, None] + rank_mine, -1
    )
    push_own = push[0][:, None]
    stay = jnp.where(sent & (rank_sent >= push_own), rank_sent - push_own, -1)
    moved = jnp.where(sent & (rank_sent < push_own), rank_sent, -1)
    above = jnp.concatenate([moved[1:], moved[:1]], axis=0)
    rides = (above >= 0) & (line < 14)
    spots_sent = jnp.where(rides, kept[0][:, None] + above, stay)
    table = lists_of(
        jnp.concatenate([spots_mine, spots_sent, moved[:1]], axis=0),
        jnp.concatenate([spot, jnp.broadcast_to(origin[None], (NZ + 1, NPLANE * 16))], axis=0),
        LOCAL,
    )
    recv_list = (table[:NZ] + TRASH).reshape(-1)
    send_list = table[NZ:].reshape(-1)
    at = jnp.arange(NEAR, dtype=jnp.int32)[:, None, None]
    near_hits = jnp.where(spots_near[None] == at, spot[None], 0)
    near_list = jnp.sum(near_hits, axis=(1, 2)) + TRASH
    meta = jnp.stack([me, jnp.sum(push_mine)])
    push_flat, kept_flat = push.reshape(-1), kept.reshape(-1)
    meta, recv_list, send_list, near_list, push_flat, kept_flat, crowded = lax.optimization_barrier(
        (meta, recv_list, send_list, near_list, push_flat, kept_flat, crowded)
    )

    def fast(spread):
        buf = kernel_call(
            pack_kernel,
            out_shape=shape_of(NZ * (CAP + CS), 8, 128),
            in_specs=[SMEM, SMEM, VMEM],
            out_specs=VMEM,
        )(meta, send_list, spread)
        buf = lax.all_to_all(buf, "z", 0, 0, tiled=True)
        near = kernel_call(
            relay_kernel,
            out_shape=shape_of(NEAR, 8, 128),
            in_specs=[SMEM] * 4 + [VMEM] * 2,
            out_specs=VMEM,
        )(meta, push_flat, kept_flat, send_list, spread, buf)
        near = lax.ppermute(near, "z", [(i, (i + 1) % NZ) for i in range(NZ)])
        early = kernel_call(
            early_kernel,
            out_shape=MERGED,
            in_specs=[SMEM] * 3 + [VMEM] * 2,
            out_specs=VMEM,
            scratch_shapes=[TOTAL],
        )(meta, recv_list, send_list, spread, buf)
        return kernel_call(
            late_kernel,
            out_shape=MERGED,
            in_specs=[SMEM] * 2 + [VMEM] * 2,
            out_specs=VMEM,
        )(meta, near_list, near, early)

    def full(spread):
        plane = jnp.where(dead, NZ, key & 15)
        mask = jnp.concatenate([mine, plane[0][None] == step[:, None]], axis=0)
        spots = jnp.where(mask, ranks_of(mask, before), -1)
        value = jnp.concatenate([spot, jnp.broadcast_to(origin[None], spot.shape)], axis=0)
        lists = lists_of(spots, value, FULL)
        theirs = lists[NZ:].reshape(-1)
        ours = (jnp.roll(lists[:NZ], me, axis=0) + TRASH).reshape(-1)
        buf = kernel_call(
            full_pack_kernel,
            out_shape=shape_of(NZ * (FULL + CS), 8, 128),
            in_specs=[SMEM, VMEM],
            out_specs=VMEM,
        )(theirs, spread)
        buf = lax.all_to_all(buf, "z", 0, 0, tiled=True)
        return kernel_call(
            full_gather_kernel,
            out_shape=MERGED,
            in_specs=[SMEM, SMEM, VMEM],
            out_specs=VMEM,
            scratch_shapes=[TOTAL],
        )(meta, ours, buf)

    merged = lax.cond(crowded, full, fast, spread)
    parts = lax.all_to_all(merged, PLANE, 0, 0, tiled=True)
    result = kernel_call(
        final_kernel,
        out_shape=shape_of(NQ, 128, 128),
        in_specs=[VMEM, VMEM],
        out_specs=VMEM,
    )(parts, boundary_block.reshape(NQ, 128, 128))
    return result.reshape(NQ, 128, 1, 128)


def solution(mesh):
    fine = Mesh(mesh.devices.reshape(YLO, NZ, XS, YHI, CORE), ("ylo", "z", "x", "yhi", "core"))
    row, col = ("ylo", "z"), ("x", "yhi", "core")
    return jax.shard_map(
        on_device,
        mesh=fine,
        in_specs=(
            P(),
            P(),
            P(row + col, None),
            P(row + col, None),
            P(None, row, None, col),
        ),
        out_specs=P(None, row, None, col),
        check_vma=False,
    )
```

```python
import functools

import jax
import jax.numpy as jnp
from jax import lax
from jax.experimental import pallas as pl
from jax.experimental.pallas import tpu as pltpu
from jax.sharding import Mesh, PartitionSpec as P

CS = 2
YLO, NZ, XS, YHI, CORE = 2, 16, 4, 2, 2
NCOL = XS * YHI * CORE
PLANE = ("x", "yhi", "ylo", "core")
NPLANE = YLO * NCOL
LIVE = 6
SLOTS = 2 * LIVE + CS
NQ = 24
CAP = 22
NEAR = 64
LOCAL = 40
FULL = 64
TRASH = NPLANE * NQ
VMEM = pl.BlockSpec(memory_space=pltpu.VMEM)
SMEM = pl.BlockSpec(memory_space=pltpu.SMEM)


def kernel_call(kernel, limit=16, **rest):
    params = pltpu.CompilerParams(vmem_limit_bytes=limit * 2**20)
    return pl.pallas_call(kernel, compiler_params=params, **rest)


def low_half(shape):
    return lax.broadcasted_iota(jnp.int32, shape, 0) % 8 < 4


def slice_kernel(first, second, out):
    low = low_half((128, 128))

    def put(slot, left, right):
        even = jnp.where(low, left, jnp.roll(right.reshape(16, 8, 128), 4, axis=1).reshape(128, 128))
        odd = jnp.where(low, jnp.roll(left.reshape(16, 8, 128), 4, axis=1).reshape(128, 128), right)
        even = even.reshape(16, 8, 128)
        odd = odd.reshape(16, 8, 128)
        for i in range(16):
            out[2 * i, slot] = even[i]
            out[2 * i + 1, slot] = odd[i]

    for member, tiles in enumerate((first, second)):
        for k in range(LIVE):
            rows = pl.ds((CS + k) * 128, 128)
            put(member * LIVE + k, tiles[rows, 0:128], tiles[rows, 128:256])
    for k in range(CS):
        rows = pl.ds(k * 128, 128)
        put(
            2 * LIVE + k,
            first[rows, 0:128] + second[rows, 0:128],
            first[rows, 128:256] + second[rows, 128:256],
        )


def place_of(ylo, col):
    return col // CORE * (YLO * CORE) + ylo * CORE + col % CORE


def shared_slice(slices, target, k):
    source = lax.rem(target + NZ - k, NZ)
    return (
        slices[place_of(0, source) * SLOTS + 2 * LIVE + k]
        + slices[place_of(1, source) * SLOTS + 2 * LIVE + k]
    )


def pack_kernel(meta, send_list, slices, out):
    me = meta[0]
    for code in range(NZ - 1):
        target = lax.rem(me + code + 1, NZ)
        base = target * (CAP + CS)

        def body(p, carry, code=code, base=base):
            out[base + p] = slices[send_list[code * LOCAL + p]]
            return carry

        lax.fori_loop(0, CAP, body, 0, unroll=True)
        for k in range(CS):
            out[base + CAP + k] = shared_slice(slices, target, k)


def relay_kernel(meta, push, kept, send_list, slices, buf, out):
    me = meta[0]
    count = push[0]

    def own(p, carry):
        out[p] = slices[send_list[NZ * LOCAL + p]]
        return carry

    lax.fori_loop(0, count, own, 0)
    for code in range(1, NZ - 1):
        line = NZ - code
        begin = kept[line * NZ + code - 1] + lax.rem(me + line, NZ) * (CAP + CS)
        more = push[line * NZ + code]

        def body(p, carry, begin=begin, count=count):
            out[count + p] = buf[begin + p]
            return carry

        lax.fori_loop(0, more, body, 0)
        count = count + more


def early_kernel(meta, recv_list, send_list, slices, buf, out, total):
    me = meta[0]
    total[...] = jnp.zeros_like(total)

    def body(p, carry):
        spot = recv_list[p]
        total[spot] = total[spot] + slices[send_list[15 * LOCAL + p]]
        return carry

    lax.fori_loop(0, LOCAL, body, 0, unroll=2)
    tiles = [shared_slice(slices, me, k) for k in range(CS)]
    for line in range(1, NZ):
        base = lax.rem(me + line, NZ) * (CAP + CS)

        def add(p, carry, base=base, line=line):
            spot = recv_list[line * LOCAL + p]
            total[spot] = total[spot] + buf[base + p]
            return carry

        lax.fori_loop(0, CAP, add, 0, unroll=2)
        tiles = [tile + buf[base + CAP + k] for k, tile in enumerate(tiles)]
    for k in range(CS):
        spot = lax.rem(me + NZ - k, NZ) * NQ
        total[spot] = total[spot] + tiles[k]
    merge(total, out)


def merge(total, out):
    low = low_half((8, 128))

    def body(at, carry):
        side = at // NCOL * NCOL
        left = lax.rem(at + NCOL - 1, NCOL) + side
        place = place_of(at // NCOL, at % NCOL)
        for h in range(NQ // 2):
            a0 = total[at * NQ + 2 * h]
            a1 = total[at * NQ + 2 * h + 1]
            b0 = total[left * NQ + 2 * h]
            b1 = total[left * NQ + 2 * h + 1]
            out[place, h] = jnp.where(
                low, a0 + jnp.roll(b0, 4, axis=0), jnp.roll(a1, 4, axis=0) + b1
            )
        return carry

    lax.fori_loop(0, NPLANE, body, 0)


def late_kernel(meta, near_list, near, early, out):
    out[...] = early[...]
    side = lax.broadcasted_iota(jnp.int32, (8, 128), 0) // 4

    def body(p, carry):
        spot = near_list[p]
        at, q = spot // NQ, spot % NQ
        h, odd = q // 2, q % 2
        here = place_of(at // NCOL, at % NCOL)
        right = place_of(at // NCOL, (at + 1) % NCOL)
        tile = near[p]
        turned = jnp.roll(tile, 4, axis=0)
        keep = side == odd
        first = jnp.where(odd == 0, tile, turned)
        second = jnp.where(odd == 0, turned, tile)
        out[here, h] = out[here, h] + jnp.where(keep, first, 0.0)
        out[right, h] = out[right, h] + jnp.where(keep, second, 0.0)
        return carry

    lax.fori_loop(0, meta[1], body, 0)


def full_pack_kernel(send_list, slices, out):
    def body(target, carry):
        def inner(p, carry):
            out[target * (FULL + CS) + p] = slices[send_list[target * FULL + p]]
            return carry

        lax.fori_loop(0, FULL, inner, 0)
        for k in range(CS):
            out[target * (FULL + CS) + FULL + k] = shared_slice(slices, target, k)
        return carry

    lax.fori_loop(0, NZ, body, 0)


def full_gather_kernel(meta, recv_list, buf, out, total):
    me = meta[0]
    total[...] = jnp.zeros_like(total)

    def body(source, carry):
        def inner(p, carry):
            spot = recv_list[source * FULL + p]
            total[spot] = total[spot] + buf[source * (FULL + CS) + p]
            return carry

        lax.fori_loop(0, FULL, inner, 0)
        for k in range(CS):
            spot = lax.rem(me + NZ - k, NZ) * NQ
            total[spot] = total[spot] + buf[source * (FULL + CS) + FULL + k]
        return carry

    lax.fori_loop(0, NZ, body, 0)
    merge(total, out)


def final_kernel(parts, given, out):
    low = low_half((8, 128))

    def body(h, carry):
        for half in range(2):
            base = given[2 * h + half].astype(jnp.float32)
            for i in range(16):
                a = parts[2 * i, h]
                b = parts[2 * i + 1, h]
                if half == 0:
                    tile = jnp.where(low, a, jnp.roll(b, 4, axis=0))
                else:
                    tile = jnp.where(low, jnp.roll(a, 4, axis=0), b)
                out[2 * h + half, 8 * i : 8 * i + 8, :] = base[8 * i : 8 * i + 8] - tile
        return carry

    lax.fori_loop(0, NQ // 2, body, 0)


def lists_of(spots, value, count):
    at = jnp.arange(count, dtype=jnp.int32)
    return jnp.sum(
        jnp.where(spots[:, None, :] == at[None, :, None], value[:, None, :], 0), axis=-1
    )


def shape_of(*shape):
    return jax.ShapeDtypeStruct(shape, jnp.float32)


MERGED = shape_of(NPLANE, NQ // 2, 8, 128)
TOTAL = pltpu.VMEM((TRASH + 1, 8, 128), jnp.float32)


def ranks_of(mask, before):
    rank = jnp.dot(mask.astype(jnp.bfloat16), before, preferred_element_type=jnp.float32)
    return rank.astype(jnp.int32)


def on_device(block_ids, iface_counts, inv_factor, coupling, boundary_block):
    me = lax.axis_index("z").astype(jnp.int32)
    width = inv_factor.shape[1]
    tiles = []
    for member in range(2):
        rows = slice(member * width, (member + 1) * width)
        mixed = jnp.dot(
            inv_factor[rows], coupling[rows], preferred_element_type=jnp.float32
        ).astype(jnp.bfloat16)
        tiles.append(
            lax.dot_general(
                mixed,
                mixed[:, : CS * 128],
                (((0,), (0,)), ((), ())),
                preferred_element_type=jnp.float32,
            )
        )
    slices = kernel_call(
        slice_kernel,
        out_shape=shape_of(NPLANE, SLOTS, 8, 128),
        in_specs=[VMEM, VMEM],
        out_specs=VMEM,
    )(*tiles)
    spread = lax.all_to_all(slices, PLANE, 0, 0, tiled=True).reshape(NPLANE * SLOTS, 8, 128)

    slot = jnp.arange(8, dtype=jnp.int32)
    alive = (slot[None] >= CS) & (slot[None] < iface_counts[:, None])
    key = jnp.where(alive, block_ids, -1)
    key = key.reshape(YLO, NZ, NCOL * 16).transpose(1, 0, 2).reshape(NZ, NPLANE * 16)
    key = lax.dynamic_slice_in_dim(jnp.concatenate([key, key], axis=0), me, NZ, 0)
    entry = jnp.arange(NPLANE * 16, dtype=jnp.int32)
    before = (entry[:, None] < entry[None, :]).astype(jnp.bfloat16)
    step = jnp.arange(NZ, dtype=jnp.int32)
    line, code = step[:, None], step[None, :]
    spot = (((key >> 4) & 1) * NCOL + ((entry >> 4) & 15)[None]) * NQ + (key >> 5) - TRASH
    origin = place_of(entry >> 8, (entry >> 4) & 15) * SLOTS + ((entry >> 3) & 1) * LIVE + (entry & 7) - CS
    dead = key < 0
    hop = (key - me - line) & 15
    turn = jnp.where(dead, -1, (hop - 1) & 15)
    load = jnp.sum((turn[:, None, :] == step[None, :, None]).astype(jnp.int32), axis=-1)

    inner = step[None, :] >= step[:, None]
    extra = jnp.where(code == 15, 0, load) - CAP
    run = jnp.sum(jnp.where(inner[None], extra[:, None, :], 0), axis=-1)
    push = run - jnp.minimum(jnp.min(jnp.where(inner[None], run[:, None, :], 0), axis=-1), 0)
    kept = load - push
    place = step[:, None, None]
    meets = ((place - step[None, None, :] - step[None, :, None]) & 15) == 0
    near = jnp.sum(jnp.where(meets, push[None], 0), axis=(1, 2))
    crowded = (
        (jnp.min(kept) < 0)
        | (jnp.max(near) > NEAR)
        | (jnp.max(push) > LOCAL)
        | (jnp.max(jnp.where(code == 15, load, 0)) > LOCAL)
    )

    mine = (key & 15 == me) & ~dead
    sent = turn[0][None] == step[:, None]
    rank = ranks_of(jnp.concatenate([mine, sent], axis=0), before)
    rank_mine, rank_sent = rank[:NZ], rank[NZ:]
    push_mine = jnp.sum(jnp.where(code == 15 - line, push, 0), axis=1)
    spots_mine = jnp.where(mine, rank_mine - push_mine[:, None], -1)
    base = jnp.sum(jnp.where(code > line, push_mine[None], 0), axis=1)
    spots_near = jnp.where(
        mine & (rank_mine < push_mine[:, None]), base[:, None] + rank_mine, -1
    )
    push_own = push[0][:, None]
    stay = jnp.where(sent & (rank_sent >= push_own), rank_sent - push_own, -1)
    moved = jnp.where(sent & (rank_sent < push_own), rank_sent, -1)
    above = jnp.concatenate([moved[1:], moved[:1]], axis=0)
    rides = (above >= 0) & (line < 14)
    spots_sent = jnp.where(rides, kept[0][:, None] + above, stay)
    table = lists_of(
        jnp.concatenate([spots_mine, spots_sent, moved[:1]], axis=0),
        jnp.concatenate([spot, jnp.broadcast_to(origin[None], (NZ + 1, NPLANE * 16))], axis=0),
        LOCAL,
    )
    recv_list = (table[:NZ] + TRASH).reshape(-1)
    send_list = table[NZ:].reshape(-1)
    at = jnp.arange(NEAR, dtype=jnp.int32)[:, None, None]
    near_hits = jnp.where(spots_near[None] == at, spot[None], 0)
    near_list = jnp.sum(near_hits, axis=(1, 2)) + TRASH
    meta = jnp.stack([me, jnp.sum(push_mine)])
    push_flat, kept_flat = push.reshape(-1), kept.reshape(-1)
    meta, recv_list, send_list, near_list, push_flat, kept_flat, crowded = lax.optimization_barrier(
        (meta, recv_list, send_list, near_list, push_flat, kept_flat, crowded)
    )

    def fast(spread):
        buf = kernel_call(
            pack_kernel,
            out_shape=shape_of(NZ * (CAP + CS), 8, 128),
            in_specs=[SMEM, SMEM, VMEM],
            out_specs=VMEM,
        )(meta, send_list, spread)
        buf = lax.all_to_all(buf, "z", 0, 0, tiled=True)
        near = kernel_call(
            relay_kernel,
            out_shape=shape_of(NEAR, 8, 128),
            in_specs=[SMEM] * 4 + [VMEM] * 2,
            out_specs=VMEM,
        )(meta, push_flat, kept_flat, send_list, spread, buf)
        near = lax.ppermute(near, "z", [(i, (i + 1) % NZ) for i in range(NZ)])
        early = kernel_call(
            early_kernel,
            out_shape=MERGED,
            in_specs=[SMEM] * 3 + [VMEM] * 2,
            out_specs=VMEM,
            scratch_shapes=[TOTAL],
        )(meta, recv_list, send_list, spread, buf)
        return kernel_call(
            late_kernel,
            out_shape=MERGED,
            in_specs=[SMEM] * 2 + [VMEM] * 2,
            out_specs=VMEM,
        )(meta, near_list, near, early)

    def full(spread):
        plane = jnp.where(dead, NZ, key & 15)
        mask = jnp.concatenate([mine, plane[0][None] == step[:, None]], axis=0)
        spots = jnp.where(mask, ranks_of(mask, before), -1)
        value = jnp.concatenate([spot, jnp.broadcast_to(origin[None], spot.shape)], axis=0)
        lists = lists_of(spots, value, FULL)
        theirs = lists[NZ:].reshape(-1)
        ours = (jnp.roll(lists[:NZ], me, axis=0) + TRASH).reshape(-1)
        buf = kernel_call(
            full_pack_kernel,
            out_shape=shape_of(NZ * (FULL + CS), 8, 128),
            in_specs=[SMEM, VMEM],
            out_specs=VMEM,
        )(theirs, spread)
        buf = lax.all_to_all(buf, "z", 0, 0, tiled=True)
        return kernel_call(
            full_gather_kernel,
            out_shape=MERGED,
            in_specs=[SMEM, SMEM, VMEM],
            out_specs=VMEM,
            scratch_shapes=[TOTAL],
        )(meta, ours, buf)

    merged = lax.cond(crowded, full, fast, spread)
    parts = lax.all_to_all(merged, PLANE, 0, 0, tiled=True)
    result = kernel_call(
        final_kernel,
        out_shape=shape_of(NQ, 128, 128),
        in_specs=[VMEM, VMEM],
        out_specs=VMEM,
    )(parts, boundary_block.reshape(NQ, 128, 128))
    return result.reshape(NQ, 128, 1, 128)


def solution(mesh):
    fine = Mesh(mesh.devices.reshape(YLO, NZ, XS, YHI, CORE), ("ylo", "z", "x", "yhi", "core"))
    row, col = ("ylo", "z"), ("x", "yhi", "core")
    return jax.shard_map(
        on_device,
        mesh=fine,
        in_specs=(
            P(),
            P(),
            P(row + col, None),
            P(row + col, None),
            P(None, row, None, col),
        ),
        out_specs=P(None, row, None, col),
        check_vma=False,
    )
```

```python
import functools

import jax
import jax.numpy as jnp
from jax import lax
from jax.experimental import pallas as pl
from jax.experimental.pallas import tpu as pltpu
from jax.sharding import Mesh, PartitionSpec as P

CS = 2
YLO, NZ, XS, YHI, CORE = 2, 16, 4, 2, 2
NCOL = XS * YHI * CORE
PLANE = ("x", "yhi", "ylo", "core")
NPLANE = YLO * NCOL
LIVE = 6
SLOTS = 2 * LIVE + CS
NQ = 24
CAP = 22
NEAR = 56
LOCAL = 40
FULL = 64
TRASH = NPLANE * NQ
VMEM = pl.BlockSpec(memory_space=pltpu.VMEM)
SMEM = pl.BlockSpec(memory_space=pltpu.SMEM)


def kernel_call(kernel, limit=16, **rest):
    params = pltpu.CompilerParams(vmem_limit_bytes=limit * 2**20)
    return pl.pallas_call(kernel, compiler_params=params, **rest)


def low_half(shape):
    return lax.broadcasted_iota(jnp.int32, shape, 0) % 8 < 4


def slice_kernel(first, second, out):
    low = low_half((128, 128))

    def put(slot, left, right):
        even = jnp.where(low, left, jnp.roll(right.reshape(16, 8, 128), 4, axis=1).reshape(128, 128))
        odd = jnp.where(low, jnp.roll(left.reshape(16, 8, 128), 4, axis=1).reshape(128, 128), right)
        even = even.reshape(16, 8, 128)
        odd = odd.reshape(16, 8, 128)
        for i in range(16):
            out[2 * i, slot] = even[i]
            out[2 * i + 1, slot] = odd[i]

    for member, tiles in enumerate((first, second)):
        for k in range(LIVE):
            rows = pl.ds((CS + k) * 128, 128)
            put(member * LIVE + k, tiles[rows, 0:128], tiles[rows, 128:256])
    for k in range(CS):
        rows = pl.ds(k * 128, 128)
        put(
            2 * LIVE + k,
            first[rows, 0:128] + second[rows, 0:128],
            first[rows, 128:256] + second[rows, 128:256],
        )


def place_of(ylo, col):
    return col // CORE * (YLO * CORE) + ylo * CORE + col % CORE


def shared_slice(slices, target, k):
    source = lax.rem(target + NZ - k, NZ)
    return (
        slices[place_of(0, source) * SLOTS + 2 * LIVE + k]
        + slices[place_of(1, source) * SLOTS + 2 * LIVE + k]
    )


def pack_kernel(meta, send_list, slices, out):
    me = meta[0]
    for code in range(NZ - 1):
        target = lax.rem(me + code + 1, NZ)
        base = target * (CAP + CS)

        def body(p, carry, code=code, base=base):
            out[base + p] = slices[send_list[code * LOCAL + p]]
            return carry

        lax.fori_loop(0, CAP, body, 0, unroll=True)
        for k in range(CS):
            out[base + CAP + k] = shared_slice(slices, target, k)


def relay_kernel(meta, push, kept, send_list, slices, buf, out):
    me = meta[0]
    count = push[0]

    def own(p, carry):
        out[p] = slices[send_list[NZ * LOCAL + p]]
        return carry

    lax.fori_loop(0, count, own, 0)
    for code in range(1, NZ - 1):
        line = NZ - code
        begin = kept[line * NZ + code - 1] + lax.rem(me + line, NZ) * (CAP + CS)
        more = push[line * NZ + code]

        def body(p, carry, begin=begin, count=count):
            out[count + p] = buf[begin + p]
            return carry

        lax.fori_loop(0, more, body, 0)
        count = count + more


def early_kernel(meta, recv_list, send_list, slices, buf, out, total):
    me = meta[0]
    total[...] = jnp.zeros_like(total)

    def body(p, carry):
        spot = recv_list[p]
        total[spot] = total[spot] + slices[send_list[15 * LOCAL + p]]
        return carry

    lax.fori_loop(0, LOCAL, body, 0, unroll=2)
    tiles = [shared_slice(slices, me, k) for k in range(CS)]
    for line in range(1, NZ):
        base = lax.rem(me + line, NZ) * (CAP + CS)

        def add(p, carry, base=base, line=line):
            spot = recv_list[line * LOCAL + p]
            total[spot] = total[spot] + buf[base + p]
            return carry

        lax.fori_loop(0, CAP, add, 0, unroll=2)
        tiles = [tile + buf[base + CAP + k] for k, tile in enumerate(tiles)]
    for k in range(CS):
        spot = lax.rem(me + NZ - k, NZ) * NQ
        total[spot] = total[spot] + tiles[k]
    merge(total, out)


def merge(total, out):
    low = low_half((8, 128))

    def body(at, carry):
        side = at // NCOL * NCOL
        left = lax.rem(at + NCOL - 1, NCOL) + side
        place = place_of(at // NCOL, at % NCOL)
        for h in range(NQ // 2):
            a0 = total[at * NQ + 2 * h]
            a1 = total[at * NQ + 2 * h + 1]
            b0 = total[left * NQ + 2 * h]
            b1 = total[left * NQ + 2 * h + 1]
            out[place, h] = jnp.where(
                low, a0 + jnp.roll(b0, 4, axis=0), jnp.roll(a1, 4, axis=0) + b1
            )
        return carry

    lax.fori_loop(0, NPLANE, body, 0)


def late_kernel(meta, near_list, near, early, out):
    out[...] = early[...]
    side = lax.broadcasted_iota(jnp.int32, (8, 128), 0) // 4

    def body(p, carry):
        spot = near_list[p]
        at, q = spot // NQ, spot % NQ
        h, odd = q // 2, q % 2
        here = place_of(at // NCOL, at % NCOL)
        right = place_of(at // NCOL, (at + 1) % NCOL)
        tile = near[p]
        turned = jnp.roll(tile, 4, axis=0)
        keep = side == odd
        first = jnp.where(odd == 0, tile, turned)
        second = jnp.where(odd == 0, turned, tile)
        out[here, h] = out[here, h] + jnp.where(keep, first, 0.0)
        out[right, h] = out[right, h] + jnp.where(keep, second, 0.0)
        return carry

    lax.fori_loop(0, meta[1], body, 0)


def full_pack_kernel(send_list, slices, out):
    def body(target, carry):
        def inner(p, carry):
            out[target * (FULL + CS) + p] = slices[send_list[target * FULL + p]]
            return carry

        lax.fori_loop(0, FULL, inner, 0)
        for k in range(CS):
            out[target * (FULL + CS) + FULL + k] = shared_slice(slices, target, k)
        return carry

    lax.fori_loop(0, NZ, body, 0)


def full_gather_kernel(meta, recv_list, buf, out, total):
    me = meta[0]
    total[...] = jnp.zeros_like(total)

    def body(source, carry):
        def inner(p, carry):
            spot = recv_list[source * FULL + p]
            total[spot] = total[spot] + buf[source * (FULL + CS) + p]
            return carry

        lax.fori_loop(0, FULL, inner, 0)
        for k in range(CS):
            spot = lax.rem(me + NZ - k, NZ) * NQ
            total[spot] = total[spot] + buf[source * (FULL + CS) + FULL + k]
        return carry

    lax.fori_loop(0, NZ, body, 0)
    merge(total, out)


def final_kernel(parts, given, out):
    low = low_half((8, 128))

    def body(h, carry):
        for half in range(2):
            base = given[2 * h + half].astype(jnp.float32)
            for i in range(16):
                a = parts[2 * i, h]
                b = parts[2 * i + 1, h]
                if half == 0:
                    tile = jnp.where(low, a, jnp.roll(b, 4, axis=0))
                else:
                    tile = jnp.where(low, jnp.roll(a, 4, axis=0), b)
                out[2 * h + half, 8 * i : 8 * i + 8, :] = base[8 * i : 8 * i + 8] - tile
        return carry

    lax.fori_loop(0, NQ // 2, body, 0)


def lists_of(spots, value, count):
    at = jnp.arange(count, dtype=jnp.int32)
    return jnp.sum(
        jnp.where(spots[:, None, :] == at[None, :, None], value[:, None, :], 0), axis=-1
    )


def shape_of(*shape):
    return jax.ShapeDtypeStruct(shape, jnp.float32)


MERGED = shape_of(NPLANE, NQ // 2, 8, 128)
TOTAL = pltpu.VMEM((TRASH + 1, 8, 128), jnp.float32)


def ranks_of(mask, before):
    rank = jnp.dot(mask.astype(jnp.bfloat16), before, preferred_element_type=jnp.float32)
    return rank.astype(jnp.int32)


def on_device(block_ids, iface_counts, inv_factor, coupling, boundary_block):
    me = lax.axis_index("z").astype(jnp.int32)
    width = inv_factor.shape[1]
    tiles = []
    for member in range(2):
        rows = slice(member * width, (member + 1) * width)
        mixed = jnp.dot(
            inv_factor[rows], coupling[rows], preferred_element_type=jnp.float32
        ).astype(jnp.bfloat16)
        tiles.append(
            lax.dot_general(
                mixed,
                mixed[:, : CS * 128],
                (((0,), (0,)), ((), ())),
                preferred_element_type=jnp.float32,
            )
        )
    slices = kernel_call(
        slice_kernel,
        out_shape=shape_of(NPLANE, SLOTS, 8, 128),
        in_specs=[VMEM, VMEM],
        out_specs=VMEM,
    )(*tiles)
    spread = lax.all_to_all(slices, PLANE, 0, 0, tiled=True).reshape(NPLANE * SLOTS, 8, 128)

    slot = jnp.arange(8, dtype=jnp.int32)
    alive = (slot[None] >= CS) & (slot[None] < iface_counts[:, None])
    key = jnp.where(alive, block_ids, -1)
    key = key.reshape(YLO, NZ, NCOL * 16).transpose(1, 0, 2).reshape(NZ, NPLANE * 16)
    key = lax.dynamic_slice_in_dim(jnp.concatenate([key, key], axis=0), me, NZ, 0)
    entry = jnp.arange(NPLANE * 16, dtype=jnp.int32)
    before = (entry[:, None] < entry[None, :]).astype(jnp.bfloat16)
    step = jnp.arange(NZ, dtype=jnp.int32)
    line, code = step[:, None], step[None, :]
    spot = (((key >> 4) & 1) * NCOL + ((entry >> 4) & 15)[None]) * NQ + (key >> 5) - TRASH
    origin = place_of(entry >> 8, (entry >> 4) & 15) * SLOTS + ((entry >> 3) & 1) * LIVE + (entry & 7) - CS
    dead = key < 0
    hop = (key - me - line) & 15
    turn = jnp.where(dead, -1, (hop - 1) & 15)
    load = jnp.sum((turn[:, None, :] == step[None, :, None]).astype(jnp.int32), axis=-1)

    inner = step[None, :] >= step[:, None]
    extra = jnp.where(code == 15, 0, load) - CAP
    run = jnp.sum(jnp.where(inner[None], extra[:, None, :], 0), axis=-1)
    push = run - jnp.minimum(jnp.min(jnp.where(inner[None], run[:, None, :], 0), axis=-1), 0)
    kept = load - push
    place = step[:, None, None]
    meets = ((place - step[None, None, :] - step[None, :, None]) & 15) == 0
    near = jnp.sum(jnp.where(meets, push[None], 0), axis=(1, 2))
    crowded = (
        (jnp.min(kept) < 0)
        | (jnp.max(near) > NEAR)
        | (jnp.max(push) > LOCAL)
        | (jnp.max(jnp.where(code == 15, load, 0)) > LOCAL)
    )

    mine = (key & 15 == me) & ~dead
    sent = turn[0][None] == step[:, None]
    rank = ranks_of(jnp.concatenate([mine, sent], axis=0), before)
    rank_mine, rank_sent = rank[:NZ], rank[NZ:]
    push_mine = jnp.sum(jnp.where(code == 15 - line, push, 0), axis=1)
    spots_mine = jnp.where(mine, rank_mine - push_mine[:, None], -1)
    base = jnp.sum(jnp.where(code > line, push_mine[None], 0), axis=1)
    spots_near = jnp.where(
        mine & (rank_mine < push_mine[:, None]), base[:, None] + rank_mine, -1
    )
    push_own = push[0][:, None]
    stay = jnp.where(sent & (rank_sent >= push_own), rank_sent - push_own, -1)
    moved = jnp.where(sent & (rank_sent < push_own), rank_sent, -1)
    above = jnp.concatenate([moved[1:], moved[:1]], axis=0)
    rides = (above >= 0) & (line < 14)
    spots_sent = jnp.where(rides, kept[0][:, None] + above, stay)
    table = lists_of(
        jnp.concatenate([spots_mine, spots_sent, moved[:1]], axis=0),
        jnp.concatenate([spot, jnp.broadcast_to(origin[None], (NZ + 1, NPLANE * 16))], axis=0),
        LOCAL,
    )
    recv_list = (table[:NZ] + TRASH).reshape(-1)
    send_list = table[NZ:].reshape(-1)
    at = jnp.arange(NEAR, dtype=jnp.int32)[:, None, None]
    near_hits = jnp.where(spots_near[None] == at, spot[None], 0)
    near_list = jnp.sum(near_hits, axis=(1, 2)) + TRASH
    meta = jnp.stack([me, jnp.sum(push_mine)])
    push_flat, kept_flat = push.reshape(-1), kept.reshape(-1)
    meta, recv_list, send_list, near_list, push_flat, kept_flat, crowded = lax.optimization_barrier(
        (meta, recv_list, send_list, near_list, push_flat, kept_flat, crowded)
    )

    def fast(spread):
        buf = kernel_call(
            pack_kernel,
            out_shape=shape_of(NZ * (CAP + CS), 8, 128),
            in_specs=[SMEM, SMEM, VMEM],
            out_specs=VMEM,
        )(meta, send_list, spread)
        buf = lax.all_to_all(buf, "z", 0, 0, tiled=True)
        near = kernel_call(
            relay_kernel,
            out_shape=shape_of(NEAR, 8, 128),
            in_specs=[SMEM] * 4 + [VMEM] * 2,
            out_specs=VMEM,
        )(meta, push_flat, kept_flat, send_list, spread, buf)
        near = lax.ppermute(near, "z", [(i, (i + 1) % NZ) for i in range(NZ)])
        early = kernel_call(
            early_kernel,
            out_shape=MERGED,
            in_specs=[SMEM] * 3 + [VMEM] * 2,
            out_specs=VMEM,
            scratch_shapes=[TOTAL],
        )(meta, recv_list, send_list, spread, buf)
        return kernel_call(
            late_kernel,
            out_shape=MERGED,
            in_specs=[SMEM] * 2 + [VMEM] * 2,
            out_specs=VMEM,
        )(meta, near_list, near, early)

    def full(spread):
        plane = jnp.where(dead, NZ, key & 15)
        mask = jnp.concatenate([mine, plane[0][None] == step[:, None]], axis=0)
        spots = jnp.where(mask, ranks_of(mask, before), -1)
        value = jnp.concatenate([spot, jnp.broadcast_to(origin[None], spot.shape)], axis=0)
        lists = lists_of(spots, value, FULL)
        theirs = lists[NZ:].reshape(-1)
        ours = (jnp.roll(lists[:NZ], me, axis=0) + TRASH).reshape(-1)
        buf = kernel_call(
            full_pack_kernel,
            out_shape=shape_of(NZ * (FULL + CS), 8, 128),
            in_specs=[SMEM, VMEM],
            out_specs=VMEM,
        )(theirs, spread)
        buf = lax.all_to_all(buf, "z", 0, 0, tiled=True)
        return kernel_call(
            full_gather_kernel,
            out_shape=MERGED,
            in_specs=[SMEM, SMEM, VMEM],
            out_specs=VMEM,
            scratch_shapes=[TOTAL],
        )(meta, ours, buf)

    merged = lax.cond(crowded, full, fast, spread)
    parts = lax.all_to_all(merged, PLANE, 0, 0, tiled=True)
    result = kernel_call(
        final_kernel,
        out_shape=shape_of(NQ, 128, 128),
        in_specs=[VMEM, VMEM],
        out_specs=VMEM,
    )(parts, boundary_block.reshape(NQ, 128, 128))
    return result.reshape(NQ, 128, 1, 128)


def solution(mesh):
    fine = Mesh(mesh.devices.reshape(YLO, NZ, XS, YHI, CORE), ("ylo", "z", "x", "yhi", "core"))
    row, col = ("ylo", "z"), ("x", "yhi", "core")
    return jax.shard_map(
        on_device,
        mesh=fine,
        in_specs=(
            P(),
            P(),
            P(row + col, None),
            P(row + col, None),
            P(None, row, None, col),
        ),
        out_specs=P(None, row, None, col),
        check_vma=False,
    )
```
